32 devices in a mesh: row: 2 (over x), col: 8 (over z, core), depth: 2 (over y).
Axes of the slice: x: 2, y: 2, z: 4, core: 2. Of those that a mesh axis runs over, the one named last changes fastest.
Arguments:
- pair_blocks: bfloat16 [416, 128, 128], P(('row', 'col', 'depth')), may hold values from -0.375 to 0.375
- dest_owner: int32 [416, 1], P(('row', 'col', 'depth')), may hold values from 0 to 7; in each aligned block of 13 rows (0 to 12, 13 to 25, ...) at most 2 rows name the same one
- dest_tile: int32 [416], P(('row', 'col', 'depth')), may hold values from 0 to 63
- chemical_potential: float32 [1], replicated, may hold values from 0.2 to 0.8
Outputs:
- sign_step: float32 [4096, 4096], P('row', 'col')
The draws below stay inside these ranges and needn't reach their ends.
Inputs may be any that keep to these rules, and one draw needn't show every extreme that they name: `dest_owner`: among the 13 pair blocks of one device, no destination col index appears more than 2 times, a bound that some block reaches.
All inputs are finite; a program needn't handle non-finite values.
Results may differ from the reference program's by a relative error of at most 0.0038.
Values may be sent and summed in bfloat16 or wider, within the bound.
A program may use at most 64 MiB of HBM per device.

```python
import math
import jax
import jax.numpy as jnp
import numpy as np
from jax import lax

TILE = 128
TC = 4
P_DEV = 13
CAP = 2
TR = 16
ORDER = 4096
BLOCKS = 416
N_COL = 8
N_DEPTH = 2


def place_ends(entries, key, low, top_value):
    spot = [jax.random.randint(jax.random.fold_in(key, axis), (), 0, length) for axis, length in enumerate(entries.shape)]
    widest = entries.shape.index(max(entries.shape))
    neighbour = spot[:widest] + [(spot[widest] + 1) % entries.shape[widest]] + spot[widest + 1:]
    return entries.at[tuple(spot)].set(low).at[tuple(neighbour)].set(top_value)


def level_of(rng, extent, shards, smallest, top_value):
    gain, own = 1.0, jax.random.fold_in(rng, 6)
    for position, shards_of in shards:
        steps = jnp.exp(jax.random.uniform(jax.random.fold_in(own, position), (shards_of,), jnp.float32, smallest / len(shards), top_value / len(shards)))
        gain = gain * jnp.repeat(steps, extent[position] // shards_of).reshape([-1 if axis == position else 1 for axis in range(len(extent))])
    return gain


def shared_out(key, own, number, rows, amount, top, limit, skew):
    ranking = jax.random.permutation(key, amount)
    packed, ordinary = shares(amount, rows * top, limit, skew, True), shares(amount, rows * top, limit, skew, False)
    places = jnp.arange(amount)

    def named(tallies, rotation):
        used = int((tallies > 0).sum())
        fixed = max(1, used // 4)
        shifted = fixed + (places - fixed + rotation * (used - fixed)) % max(1, amount - fixed)
        return jnp.zeros((amount,), jnp.int32).at[ranking[jnp.where(places < fixed, places, shifted)]].set(jnp.asarray(tallies, jnp.int32))

    tallies = jnp.where(number % 4 == 0, named(packed, number // 4), named(ordinary, number - number // 4 - 1))
    mixed = jax.random.permutation(jax.random.fold_in(own, 3), amount)
    source_of, receiver = mixed[0:amount // 2 * 2:2], mixed[1:amount // 2 * 2:2]
    slack = jnp.minimum(tallies[source_of] - 1, limit - tallies[receiver]) // 2
    slack = jnp.where((source_of == ranking[0]) | (receiver == ranking[0]) | (tallies[receiver] == 0), 0, jnp.maximum(slack, 0))
    shifted = jax.random.randint(jax.random.fold_in(own, 4), (amount // 2,), 0, 1 << 20) % (slack + 1)
    tallies = tallies.at[source_of].add(-shifted).at[receiver].add(shifted)
    labels = jnp.searchsorted(jnp.cumsum(tallies), jnp.arange(rows * top), side="right").astype(jnp.int32)
    listing = labels.reshape(top, rows).T
    listing = listing[jax.random.permutation(jax.random.fold_in(own, 1), rows)]
    rotation = jax.random.randint(jax.random.fold_in(own, 2), (rows, 1), 0, top)
    return jnp.take_along_axis(listing, (jnp.arange(top)[None, :] + rotation) % top, axis=1)


def shares(number_of, total, bound, skew, full):
    loads = [(1 << 20) // math.isqrt(rank ** skew) + 1 for rank in range(1, number_of + 1)]
    largest = bound if full else min(bound, max(-(-total // number_of), total * loads[0] // sum(loads)))
    least = 1 if total - largest >= number_of - 1 else 0
    given, surplus = [largest] + [least] * (number_of - 1), total - largest - least * (number_of - 1)
    while surplus > 0:
        movable = [i for i in range(1, number_of) if given[i] < largest] or [i for i in range(1, number_of) if given[i] < bound]
        pool, left = sum([loads[i] for i in movable]), surplus
        for i in movable:
            more = min(bound - given[i], max(1, left * loads[i] // pool), surplus)
            given[i] = given[i] + more
            surplus = surplus - more
    return np.array(given)


def centred(key, extent, deviation, reach, pieces=(), kind=jnp.bfloat16):
    factor_of = level_of(key, extent, pieces, -0.22, 0.18) if pieces else 1.0
    drawn = jax.random.normal(key, extent, jnp.float32) * deviation * factor_of
    return jnp.minimum(jnp.maximum(drawn, -reach), reach).astype(kind)


def setup_inputs(seed: int = 0) -> dict:
    keys = jax.random.split(jax.random.key(seed), 5)
    pair_blocks = centred(keys[0], (BLOCKS, TILE, TILE), ((TR / (N_COL * N_DEPTH * P_DEV * TILE)) ** 0.5), 0.375, ((0, 32),))
    dest_owner_keys = jax.random.split(jax.random.fold_in(keys[1], 1), BLOCKS // P_DEV)
    dest_owner_turns = jax.random.permutation(jax.random.fold_in(keys[1], 3), BLOCKS // P_DEV)
    dest_owner = jax.vmap(lambda own, number: shared_out(jax.random.fold_in(keys[1], 2), own, number, P_DEV, N_COL, 1, CAP, 2))(dest_owner_keys, dest_owner_turns).reshape((BLOCKS, 1))
    dest_tile = place_ends(jax.random.randint(keys[2], (BLOCKS,), 0, TR * TC), jax.random.fold_in(keys[2], 1), 0, (TR * TC) - 1).astype(jnp.int32)
    chemical_potential = jnp.clip(jax.random.uniform(keys[3], (1,), jnp.float32, 0.2, 0.8), 0.2, 0.8)
    return {"pair_blocks": pair_blocks, "dest_owner": dest_owner, "dest_tile": dest_tile, "chemical_potential": chemical_potential}


def reference(pair_blocks, dest_owner, dest_tile, chemical_potential):
    grid_tiles = ORDER // TILE
    block_index = jnp.arange(BLOCKS, dtype=jnp.int32)
    device_index = block_index // P_DEV
    row_index = device_index // (N_COL * N_DEPTH)
    tile_row = row_index * TR + dest_tile.astype(jnp.int32) // TC
    tile_col = dest_owner[:, 0].astype(jnp.int32) * TC + dest_tile.astype(jnp.int32) % TC
    flat_index = (tile_row * grid_tiles + tile_col).astype(jnp.int32)
    assembled = jax.ops.segment_sum(pair_blocks.astype(jnp.float32), flat_index, num_segments=grid_tiles * grid_tiles)
    hamiltonian = assembled.reshape(grid_tiles, grid_tiles, TILE, TILE).transpose(0, 2, 1, 3).reshape(ORDER, ORDER)
    identity = jnp.eye(ORDER, dtype=jnp.float32)
    left_matrix = (hamiltonian - chemical_potential[0] * identity).astype(jnp.bfloat16)
    left_wide = left_matrix.astype(jnp.float32)
    squared = jnp.dot(left_wide, left_wide, precision=lax.Precision.HIGHEST)
    right_matrix = (3.0 * identity - squared).astype(jnp.bfloat16)
    return 0.5 * jnp.dot(left_wide, right_matrix.astype(jnp.float32), precision=lax.Precision.HIGHEST)
```

```python
import functools

import jax
import jax.numpy as jnp
from jax import lax
from jax.experimental import pallas as pl
from jax.experimental.pallas import tpu as pltpu
from jax.sharding import PartitionSpec as P

TC = 4
CAP = 2
TILE = 128
LABEL_ROWS = 16


def assemble(received, labels, tile_count):
    one_hot = (
        labels.astype(jnp.float32)[None, :] == jnp.arange(tile_count, dtype=jnp.float32)[:, None]
    ).astype(jnp.bfloat16)
    return jnp.dot(one_hot, received, preferred_element_type=jnp.float32)


def product(left_matrix, right_matrix):
    layer_count = lax.axis_size("depth")
    layer_index = lax.axis_index("depth")
    rows_local, cols_local = left_matrix.shape
    half_rows = rows_local // layer_count
    own_part = lax.dynamic_slice_in_dim(left_matrix, layer_index * half_rows, half_rows, 0)
    row_panel = lax.all_gather(right_matrix, "row", axis=0, tiled=True)
    partial_rows = jnp.dot(
        lax.all_gather(own_part, "col", axis=1, tiled=True),
        row_panel,
        preferred_element_type=jnp.float32,
    )
    return lax.all_gather(partial_rows, "depth", axis=0, tiled=True)


def shards(pair_blocks, dest_owner, dest_tile, chemical_potential):
    col_count = lax.axis_size("col")
    row_count = lax.axis_size("row")
    block_count = pair_blocks.shape[0]
    tile_size = pair_blocks.shape[1]
    tile_rows = TC * col_count // row_count
    tile_count = tile_rows * TC
    flat_blocks = pair_blocks.reshape(block_count, tile_size * tile_size)
    owners = dest_owner[:, 0]
    owner_hot = (owners[:, None] == jnp.arange(col_count, dtype=jnp.int32)[None, :]).astype(
        jnp.int32
    )
    earlier = jnp.cumsum(owner_hot, axis=0) - owner_hot
    slot_rank = jnp.sum(earlier * owner_hot, axis=1)
    slot_index = owners * CAP + slot_rank
    picker = (slot_index[None, :] == jnp.arange(col_count * CAP, dtype=jnp.int32)[:, None]).astype(
        jnp.int32
    )
    send_blocks = jnp.dot(
        picker.astype(jnp.bfloat16), flat_blocks, preferred_element_type=jnp.float32
    ).astype(jnp.bfloat16)
    send_blocks = send_blocks.reshape(col_count, CAP, tile_size * tile_size)
    send_labels = (
        (jnp.sum(picker * (dest_tile[None, :] + 1), axis=1) - 1)
        .astype(jnp.float32)
        .astype(jnp.bfloat16)
    )
    send_labels = send_labels.reshape(col_count, CAP)
    got_blocks, got_labels = (
        lax.all_to_all(send_blocks, "col", split_axis=0, concat_axis=0, tiled=True),
        lax.all_to_all(send_labels, "col", split_axis=0, concat_axis=0, tiled=True),
    )
    own_tiles = assemble(
        got_blocks.reshape(-1, tile_size * tile_size), got_labels.reshape(-1), tile_count
    )
    assembled = lax.psum(own_tiles, "depth")
    hamiltonian = assembled.reshape(tile_rows, TC, tile_size, tile_size).transpose(0, 2, 1, 3)
    hamiltonian = hamiltonian.reshape(tile_rows * tile_size, TC * tile_size)
    rows_local, cols_local = hamiltonian.shape
    row_first = lax.axis_index("row") * rows_local
    col_first = lax.axis_index("col") * cols_local
    identity = (
        (row_first + jnp.arange(rows_local, dtype=jnp.int32))[:, None]
        == (col_first + jnp.arange(cols_local, dtype=jnp.int32))[None, :]
    ).astype(jnp.float32)
    left_matrix = (hamiltonian - chemical_potential[0] * identity).astype(jnp.bfloat16)
    squared = product(left_matrix, left_matrix)
    right_matrix = (3.0 * identity - squared).astype(jnp.bfloat16)
    return 0.5 * product(left_matrix, right_matrix)


def gather_kernel(z_count, split, own_ref, all_ref, local_sem, send_sem, recv_sem):
    x = lax.axis_index("row")
    y = lax.axis_index("depth")
    c = lax.axis_index("col")
    z, q = c // 2, c % 2
    rows = own_ref.shape[0]
    spans = ((0, split), (split, rows - split))

    def device(px, py, pz, pq):
        return {"row": px, "col": pz * 2 + pq, "depth": py}

    def chip(px, py, pz):
        return (px * 2 + py) * z_count + pz

    z_others = [lax.rem(z + k, z_count) for k in range(1, z_count)]
    if z_count == 4:
        z_others = [z + 1 - 2 * lax.rem(z, 2), lax.rem(z + 2, 4), 3 - z]
    x_peer = device(1 - x, y, z, q)
    y_peer = device(x, 1 - y, z, q)
    sibling = device(x, y, z, 1 - q)
    peers = [device(x, y, pz, q) for pz in z_others] + [x_peer, y_peer, sibling]

    barrier = pltpu.get_barrier_semaphore()
    for peer in peers:
        pl.semaphore_signal(barrier, inc=1, device_id=peer, device_id_type=pl.DeviceIdType.MESH)
    pl.semaphore_wait(barrier, len(peers))

    started = []
    sends = [0]

    def place(source, part, parity):
        px, py, pz = source
        first, size = spans[part]
        return all_ref.at[px * (z_count * 4) + (pz * 2 + parity) * 2 + py, pl.ds(first, size)]

    def send(source, part, peer, own, to_sibling=0):
        first, size = spans[part]
        copy = pltpu.make_async_remote_copy(
            src_ref=own_ref.at[pl.ds(first, size)] if own else place(source, part, q),
            dst_ref=place(source, part, q),
            send_sem=send_sem.at[sends[0]],
            recv_sem=recv_sem.at[part, to_sibling, chip(*source)],
            device_id=peer,
            device_id_type=pl.DeviceIdType.MESH,
        )
        sends[0] += 1
        copy.start()
        started.append(copy)

    def arrived(source, part, from_sibling=0):
        parity = 1 - q if from_sibling else q
        target = place(source, part, parity)
        pltpu.make_async_remote_copy(
            src_ref=target,
            dst_ref=target,
            send_sem=send_sem.at[0],
            recv_sem=recv_sem.at[part, from_sibling, chip(*source)],
            device_id=sibling,
            device_id_type=pl.DeviceIdType.MESH,
        ).wait_recv()

    first_peer, last_peer = (x_peer, y_peer), (y_peer, x_peer)
    own = (x, y, z)
    for pz in z_others:
        for part in range(2):
            send(own, part, device(x, y, pz, q), True)
    for part in range(2):
        send(own, part, first_peer[part], True)
    for part in range(2):
        send(own, part, last_peer[part], True)
        send(own, part, sibling, True, 1)
    keep = pltpu.make_async_copy(
        own_ref, all_ref.at[x * (z_count * 4) + c * 2 + y], local_sem
    )
    keep.start()

    def second(part, pz):
        return (1 - x, y, pz) if part == 0 else (x, 1 - y, pz)

    def third(part, pz):
        return ((x, 1 - y, pz), (1 - x, 1 - y, pz)) if part == 0 else (
            (1 - x, y, pz), (1 - x, 1 - y, pz))

    order = [z] + z_others
    for step, pz in enumerate(order):
        for part in range(2):
            if step:
                arrived((x, y, pz), part)
                send((x, y, pz), part, first_peer[part], False)
                send((x, y, pz), part, last_peer[part], False)
                send((x, y, pz), part, sibling, False, 1)
        for part in range(2):
            source = second(part, pz)
            arrived(source, part)
            send(source, part, last_peer[part], False)
            send(source, part, sibling, False, 1)
    for pz in order:
        for part in range(2):
            for source in third(part, pz):
                arrived(source, part)
                send(source, part, sibling, False, 1)
    for px in range(2):
        for py in range(2):
            for pz in range(z_count):
                for part in range(2):
                    arrived((px, py, pz), part, 1)
    for copy in started:
        copy.wait_send()
    keep.wait()


def gather_pieces(piece, devices):
    rows, width = piece.shape
    z_count = lax.axis_size("col") // 2
    sends = 2 * ((z_count - 1) + 2 + (z_count - 1) * 2 + z_count + 4 * z_count)
    return pl.pallas_call(
        functools.partial(gather_kernel, z_count, (rows // 32 + 1) // 1 * 16),
        out_shape=jax.ShapeDtypeStruct((devices, rows, width), piece.dtype),
        in_specs=[pl.BlockSpec(memory_space=pl.ANY)],
        out_specs=pl.BlockSpec(memory_space=pl.ANY),
        scratch_shapes=[
            pltpu.SemaphoreType.DMA(()),
            pltpu.SemaphoreType.DMA((sends,)),
            pltpu.SemaphoreType.DMA((2, 2, 4 * z_count)),
        ],
        compiler_params=pltpu.CompilerParams(collective_id=0, has_side_effects=True),
    )(piece)


def step_kernel(
    block_count, chunk, where_ref, next_ref, place_ref, shift_ref, all_ref, out_ref,
    blocks, left, right, sem
):
    devices = all_ref.shape[0]
    order = left.shape[0]
    grid_tiles = order // TILE
    rows_local, cols_local = out_ref.shape
    shift = shift_ref[0]

    fetch = pltpu.make_async_copy(all_ref.at[:, pl.ds(0, block_count * TILE)], blocks, sem)
    fetch.start()

    eye = (
        lax.broadcasted_iota(jnp.int32, (TILE, TILE), 0)
        == lax.broadcasted_iota(jnp.int32, (TILE, TILE), 1)
    )
    shifted = jnp.where(eye, shift, 0.0)

    @pl.loop(0, grid_tiles)
    def _(i):
        rows = pl.ds(pl.multiple_of(i * TILE, TILE), TILE)
        left[rows, :] = jnp.zeros((TILE, order), left.dtype)
        left[rows, rows] = (-shifted).astype(left.dtype)

    fetch.wait()

    @pl.loop(0, devices)
    def _(g):
        for p in range(block_count):
            b = g * block_count + p
            tile = where_ref[b]
            follower = next_ref[b]
            i = tile // grid_tiles
            k = tile % grid_tiles
            plain = jnp.logical_and(follower < 0, i != k)
            rows = pl.ds(pl.multiple_of(i * TILE, TILE), TILE)
            cols = pl.ds(pl.multiple_of(k * TILE, TILE), TILE)
            own = pl.ds(p * TILE, TILE)

            @pl.when(jnp.logical_and(tile >= 0, plain))
            def _():
                left[rows, cols] = blocks[g, own, :]

            @pl.when(jnp.logical_and(tile >= 0, jnp.logical_not(plain)))
            def _():
                def more(carry):
                    return carry[0] >= 0

                def add(carry):
                    n, total = carry
                    row = pl.multiple_of((n % block_count) * TILE, TILE)
                    extra = blocks[n // block_count, pl.ds(row, TILE), :]
                    return next_ref[n], total + extra.astype(jnp.float32)

                _, total = lax.while_loop(
                    more, add, (follower, blocks[g, own, :].astype(jnp.float32))
                )
                left[rows, cols] = (total - jnp.where(i == k, shifted, 0.0)).astype(left.dtype)

    row_first = place_ref[0] * rows_local
    col_first = pl.multiple_of(place_ref[1] * cols_local, cols_local)
    columns = pl.ds(col_first, cols_local)

    @pl.loop(0, order // chunk)
    def _(m):
        first = pl.multiple_of(m * chunk, chunk)
        rows = pl.ds(first, chunk)
        squared = jnp.dot(left[rows, :], left[:, columns], preferred_element_type=jnp.float32)
        on_diagonal = (
            first + lax.broadcasted_iota(jnp.int32, (chunk, cols_local), 0)
            == col_first + lax.broadcasted_iota(jnp.int32, (chunk, cols_local), 1)
        )
        right[rows, :] = (jnp.where(on_diagonal, 3.0, 0.0) - squared).astype(right.dtype)

    @pl.loop(0, rows_local // chunk)
    def _(m):
        first = pl.multiple_of(m * chunk, chunk)
        rows = pl.ds(pl.multiple_of(row_first + first, chunk), chunk)
        out_ref[pl.ds(first, chunk), :] = 0.5 * jnp.dot(
            left[rows, :], right[...], preferred_element_type=jnp.float32
        )


def replicated(pair_blocks, dest_owner, dest_tile, chemical_potential):
    col_count = lax.axis_size("col")
    row_count = lax.axis_size("row")
    depth_count = lax.axis_size("depth")
    devices = row_count * col_count * depth_count
    block_count = pair_blocks.shape[0]
    grid_tiles = TC * col_count
    order = grid_tiles * TILE
    tile_rows = grid_tiles // row_count
    labels = jnp.zeros((LABEL_ROWS, TILE), jnp.bfloat16)
    labels = labels.at[0, :block_count].set(dest_tile.astype(jnp.bfloat16))
    labels = labels.at[1, :block_count].set(dest_owner[:, 0].astype(jnp.bfloat16))
    piece = jnp.concatenate([pair_blocks.reshape(block_count * TILE, TILE), labels], axis=0)
    pieces = gather_pieces(piece, devices)
    got = pieces[:, block_count * TILE : block_count * TILE + 2, :block_count].astype(jnp.int32)
    row_of = jnp.arange(devices, dtype=jnp.int32)[:, None] // (col_count * depth_count)
    tile_row = row_of * tile_rows + got[:, 0] // TC
    tile_col = got[:, 1] * TC + got[:, 0] % TC
    tiles = (tile_row * grid_tiles + tile_col).reshape(-1)
    total = devices * block_count
    index = jnp.arange(total, dtype=jnp.int32)
    same = tiles[:, None] == tiles[None, :]
    later = jnp.where(same & (index[None, :] > index[:, None]), index[None, :], total)
    follower = jnp.min(later, axis=1)
    follower = jnp.where(follower == total, -1, follower)
    opened = jnp.any(same & (index[None, :] < index[:, None]), axis=1)
    where = jnp.where(opened, -1, tiles)
    place = jnp.stack([lax.axis_index("row"), lax.axis_index("col")]).astype(jnp.int32)
    smem = pl.BlockSpec(memory_space=pltpu.SMEM)
    return pl.pallas_call(
        functools.partial(step_kernel, block_count, 512),
        out_shape=jax.ShapeDtypeStruct((order // row_count, order // col_count), jnp.float32),
        in_specs=[smem, smem, smem, smem, pl.BlockSpec(memory_space=pl.ANY)],
        out_specs=pl.BlockSpec(memory_space=pltpu.VMEM),
        scratch_shapes=[
            pltpu.VMEM((devices, block_count * TILE, TILE), jnp.bfloat16),
            pltpu.VMEM((order, order), jnp.bfloat16),
            pltpu.VMEM((order, order // col_count), jnp.bfloat16),
            pltpu.SemaphoreType.DMA(()),
        ],
        compiler_params=pltpu.CompilerParams(vmem_limit_bytes=60 * 2**20),
    )(where, follower, place, chemical_potential, pieces)


def solution(mesh):
    in_specs = (
        P(("row", "col", "depth"), None, None),
        P(("row", "col", "depth"), None),
        P(("row", "col", "depth")),
        P(),
    )
    out_specs = P("row", "col")
    sizes = mesh.shape
    small = sizes["row"] == 2 and sizes["depth"] == 2 and sizes["col"] == 8
    body = replicated if small else shards
    return jax.shard_map(body, mesh=mesh, in_specs=in_specs, out_specs=out_specs, check_vma=False)
```

```python
import functools

import jax
import jax.numpy as jnp
from jax import lax
from jax.experimental import pallas as pl
from jax.experimental.pallas import tpu as pltpu
from jax.sharding import PartitionSpec as P

TC = 4
CAP = 2
TILE = 128
LABEL_ROWS = 16


def assemble(received, labels, tile_count):
    one_hot = (
        labels.astype(jnp.float32)[None, :] == jnp.arange(tile_count, dtype=jnp.float32)[:, None]
    ).astype(jnp.bfloat16)
    return jnp.dot(one_hot, received, preferred_element_type=jnp.float32)


def product(left_matrix, right_matrix):
    layer_count = lax.axis_size("depth")
    layer_index = lax.axis_index("depth")
    rows_local, cols_local = left_matrix.shape
    half_rows = rows_local // layer_count
    own_part = lax.dynamic_slice_in_dim(left_matrix, layer_index * half_rows, half_rows, 0)
    row_panel = lax.all_gather(right_matrix, "row", axis=0, tiled=True)
    partial_rows = jnp.dot(
        lax.all_gather(own_part, "col", axis=1, tiled=True),
        row_panel,
        preferred_element_type=jnp.float32,
    )
    return lax.all_gather(partial_rows, "depth", axis=0, tiled=True)


def shards(pair_blocks, dest_owner, dest_tile, chemical_potential):
    col_count = lax.axis_size("col")
    row_count = lax.axis_size("row")
    block_count = pair_blocks.shape[0]
    tile_size = pair_blocks.shape[1]
    tile_rows = TC * col_count // row_count
    tile_count = tile_rows * TC
    flat_blocks = pair_blocks.reshape(block_count, tile_size * tile_size)
    owners = dest_owner[:, 0]
    owner_hot = (owners[:, None] == jnp.arange(col_count, dtype=jnp.int32)[None, :]).astype(
        jnp.int32
    )
    earlier = jnp.cumsum(owner_hot, axis=0) - owner_hot
    slot_rank = jnp.sum(earlier * owner_hot, axis=1)
    slot_index = owners * CAP + slot_rank
    picker = (slot_index[None, :] == jnp.arange(col_count * CAP, dtype=jnp.int32)[:, None]).astype(
        jnp.int32
    )
    send_blocks = jnp.dot(
        picker.astype(jnp.bfloat16), flat_blocks, preferred_element_type=jnp.float32
    ).astype(jnp.bfloat16)
    send_blocks = send_blocks.reshape(col_count, CAP, tile_size * tile_size)
    send_labels = (
        (jnp.sum(picker * (dest_tile[None, :] + 1), axis=1) - 1)
        .astype(jnp.float32)
        .astype(jnp.bfloat16)
    )
    send_labels = send_labels.reshape(col_count, CAP)
    got_blocks, got_labels = (
        lax.all_to_all(send_blocks, "col", split_axis=0, concat_axis=0, tiled=True),
        lax.all_to_all(send_labels, "col", split_axis=0, concat_axis=0, tiled=True),
    )
    own_tiles = assemble(
        got_blocks.reshape(-1, tile_size * tile_size), got_labels.reshape(-1), tile_count
    )
    assembled = lax.psum(own_tiles, "depth")
    hamiltonian = assembled.reshape(tile_rows, TC, tile_size, tile_size).transpose(0, 2, 1, 3)
    hamiltonian = hamiltonian.reshape(tile_rows * tile_size, TC * tile_size)
    rows_local, cols_local = hamiltonian.shape
    row_first = lax.axis_index("row") * rows_local
    col_first = lax.axis_index("col") * cols_local
    identity = (
        (row_first + jnp.arange(rows_local, dtype=jnp.int32))[:, None]
        == (col_first + jnp.arange(cols_local, dtype=jnp.int32))[None, :]
    ).astype(jnp.float32)
    left_matrix = (hamiltonian - chemical_potential[0] * identity).astype(jnp.bfloat16)
    squared = product(left_matrix, left_matrix)
    right_matrix = (3.0 * identity - squared).astype(jnp.bfloat16)
    return 0.5 * product(left_matrix, right_matrix)


def gather_kernel(spans, own_ref, all_ref, local_sem, send_sem, recv_sem):
    x = lax.axis_index("row")
    y = lax.axis_index("depth")
    c = lax.axis_index("col")
    z, q = c // 2, c % 2
    near = z + 1 - 2 * (z % 2)
    mid = (z + 2) % 4
    far = 3 - z
    inner = jnp.logical_or(z == 1, z == 2)

    def device(px, py, pz, pq):
        return {"row": px, "col": pz * 2 + pq, "depth": py}

    def chip(px, py, pz):
        return (px * 2 + py) * 4 + pz

    x_peer = device(1 - x, y, z, q)
    y_peer = device(x, 1 - y, z, q)
    sibling = device(x, y, z, 1 - q)
    near_peer, mid_peer, far_peer = (device(x, y, pz, q) for pz in (near, mid, far))
    peers = [near_peer, mid_peer, far_peer, x_peer, y_peer, sibling]

    barrier = pltpu.get_barrier_semaphore()
    for peer in peers:
        pl.semaphore_signal(barrier, inc=1, device_id=peer, device_id_type=pl.DeviceIdType.MESH)
    pl.semaphore_wait(barrier, len(peers))

    always, sometimes = [], []
    own = (x, y, z)

    def place(source, part, parity):
        px, py, pz = source
        first, size = spans[part]
        return all_ref.at[px * 16 + (pz * 2 + parity) * 2 + py, pl.ds(first, size)]

    def remote(source, part, peer, to_sibling=0):
        first, size = spans[part]
        return pltpu.make_async_remote_copy(
            src_ref=own_ref.at[pl.ds(first, size)] if source is own else place(source, part, q),
            dst_ref=place(source, part, q),
            send_sem=send_sem.at[len(always) + len(sometimes)],
            recv_sem=recv_sem.at[part, to_sibling, chip(*source)],
            device_id=peer,
            device_id_type=pl.DeviceIdType.MESH,
        )

    def send(source, part, peer, to_sibling=0):
        copy = remote(source, part, peer, to_sibling)
        copy.start()
        always.append(copy)

    def send_inner(source, part, peer):
        copy = remote(source, part, peer)
        sometimes.append(copy)

        @pl.when(inner)
        def _():
            copy.start()

    def share(source, part):
        send(source, part, sibling, 1)

    def arrived(source, part, from_sibling=0):
        target = place(source, part, 1 - q if from_sibling else q)
        pltpu.make_async_remote_copy(
            src_ref=target,
            dst_ref=target,
            send_sem=send_sem.at[0],
            recv_sem=recv_sem.at[part, from_sibling, chip(*source)],
            device_id=sibling,
            device_id_type=pl.DeviceIdType.MESH,
        ).wait_recv()

    first_peer, last_peer = (x_peer, y_peer), (y_peer, x_peer)

    def over_first(part, pz):
        return (1 - x, y, pz) if part == 0 else (x, 1 - y, pz)

    def over_last(part, pz):
        return (x, 1 - y, pz) if part == 0 else (1 - x, y, pz)

    def along_z(source):
        send(source, 2, near_peer)
        send(source, 2, mid_peer)
        send_inner(source, 2, far_peer)

    for part in range(2):
        send(own, part, mid_peer)
        send(own, part, near_peer)
        send_inner(own, part, far_peer)
    for part in range(2):
        send(own, part, first_peer[part])
    send(own, 2, x_peer)
    send(own, 2, y_peer)
    for part in range(2):
        send(own, part, last_peer[part])
    for part in range(3):
        share(own, part)
    keep = pltpu.make_async_copy(own_ref, all_ref.at[x * 16 + c * 2 + y], local_sem)
    keep.start()

    flats = [own, (1 - x, y, z), (x, 1 - y, z), (1 - x, 1 - y, z)]
    for step, pz in enumerate((z, near, mid, far)):
        for part in range(2):
            if step:
                source = (x, y, pz)
                arrived(source, part)
                if step == 2:
                    send_inner(source, part, near_peer)
                send(source, part, first_peer[part])
                send(source, part, last_peer[part])
                share(source, part)
        if step:
            flat = flats[step]
            arrived(flat, 2)
            if step == 1:
                send(flat, 2, y_peer)
                along_z(own)
            share(flat, 2)
            along_z(flat)
        for part in range(2):
            source = over_first(part, pz)
            arrived(source, part)
            send(source, part, last_peer[part])
            share(source, part)
    for step, pz in enumerate((z, mid, near, far)):
        if step:
            for px, py, _ in flats:
                source = (px, py, pz)
                arrived(source, 2)
                if step == 1:
                    send_inner(source, 2, near_peer)
                share(source, 2)
        for part in range(2):
            for source in (over_last(part, pz), (1 - x, 1 - y, pz)):
                arrived(source, part)
                share(source, part)
    for px in range(2):
        for py in range(2):
            for pz in range(4):
                for part in range(3):
                    arrived((px, py, pz), part, 1)
    for copy in always:
        copy.wait_send()
    for copy in sometimes:

        @pl.when(inner)
        def _():
            copy.wait_send()

    keep.wait()


def gather_pieces(piece, devices):
    rows, width = piece.shape
    units = rows // 16
    ends = [0, 40 * units // 105 * 16, 82 * units // 105 * 16, rows]
    spans = [(start, end - start) for start, end in zip(ends, ends[1:])]
    return pl.pallas_call(
        functools.partial(gather_kernel, spans),
        out_shape=jax.ShapeDtypeStruct((devices, rows, width), piece.dtype),
        in_specs=[pl.BlockSpec(memory_space=pl.ANY)],
        out_specs=pl.BlockSpec(memory_space=pl.ANY),
        scratch_shapes=[
            pltpu.SemaphoreType.DMA(()),
            pltpu.SemaphoreType.DMA((99,)),
            pltpu.SemaphoreType.DMA((3, 2, 16)),
        ],
        compiler_params=pltpu.CompilerParams(collective_id=0, has_side_effects=True),
    )(piece)


def step_kernel(
    block_count, chunk, row_ref, col_ref, follower_ref, chain_ref, place_ref, shift_ref, all_ref,
    out_ref, blocks, left, right, result, fetch_sem, store_sem
):
    devices = all_ref.shape[0]
    order = left.shape[0]
    grid_tiles = order // TILE
    rows_local, cols_local = out_ref.shape
    fetches = fetch_sem.shape[0]
    group = devices // fetches
    stores = store_sem.shape[0]
    slab = rows_local // stores
    shift = shift_ref[0]

    def fetch(h):
        part = pl.ds(h * group, group)
        return pltpu.make_async_copy(
            all_ref.at[part, pl.ds(0, block_count * TILE)], blocks.at[part], fetch_sem.at[h]
        )

    for h in range(fetches):
        fetch(h).start()

    eye = (
        lax.broadcasted_iota(jnp.int32, (TILE, TILE), 0)
        == lax.broadcasted_iota(jnp.int32, (TILE, TILE), 1)
    )
    shifted = jnp.where(eye, shift, 0.0)

    @pl.loop(0, grid_tiles)
    def _(i):
        rows = pl.ds(pl.multiple_of(i * TILE, TILE), TILE)
        left[rows, :] = jnp.zeros((TILE, order), left.dtype)
        left[rows, rows] = (-shifted).astype(left.dtype)

    def tile_of(b):
        return (
            pl.ds(pl.multiple_of(row_ref[b] * TILE, TILE), TILE),
            pl.ds(pl.multiple_of(col_ref[b] * TILE, TILE), TILE),
        )

    for h in range(fetches):
        fetch(h).wait()

        @pl.loop(h * group, (h + 1) * group)
        def _(g):
            for p in range(block_count):
                rows, cols = tile_of(g * block_count + p)
                left[rows, cols] = blocks[g, pl.ds(p * TILE, TILE), :]

    def block_of(b):
        row = pl.multiple_of((b % block_count) * TILE, TILE)
        return blocks[b // block_count, pl.ds(row, TILE), :].astype(jnp.float32)

    def write_sum(b):
        def add(carry):
            n, total = carry
            return follower_ref[n], total + block_of(n)

        _, total = lax.while_loop(
            lambda carry: carry[0] >= 0, add, (follower_ref[b], block_of(b))
        )
        rows, cols = tile_of(b)
        on_diagonal = row_ref[b] == col_ref[b]
        left[rows, cols] = (total - jnp.where(on_diagonal, shifted, 0.0)).astype(left.dtype)
        return chain_ref[b]

    lax.while_loop(lambda b: b < devices * block_count, write_sum, place_ref[2])

    row_first = place_ref[0] * rows_local
    col_first = pl.multiple_of(place_ref[1] * cols_local, cols_local)
    columns = pl.ds(col_first, cols_local)

    @pl.loop(0, order // chunk)
    def _(m):
        first = pl.multiple_of(m * chunk, chunk)
        rows = pl.ds(first, chunk)
        squared = jnp.dot(left[rows, :], left[:, columns], preferred_element_type=jnp.float32)
        on_diagonal = (
            first + lax.broadcasted_iota(jnp.int32, (chunk, cols_local), 0)
            == col_first + lax.broadcasted_iota(jnp.int32, (chunk, cols_local), 1)
        )
        right[rows, :] = (jnp.where(on_diagonal, 3.0, 0.0) - squared).astype(right.dtype)

    def store(m):
        part = pl.ds(m * slab, slab)
        return pltpu.make_async_copy(result.at[part], out_ref.at[part], store_sem.at[m])

    for m in range(stores):
        rows = pl.ds(pl.multiple_of(row_first + m * slab, slab), slab)
        result[pl.ds(m * slab, slab), :] = 0.5 * jnp.dot(
            left[rows, :], right[...], preferred_element_type=jnp.float32
        )
        store(m).start()
    for m in range(stores):
        store(m).wait()


def replicated(pair_blocks, dest_owner, dest_tile, chemical_potential):
    col_count = lax.axis_size("col")
    row_count = lax.axis_size("row")
    depth_count = lax.axis_size("depth")
    devices = row_count * col_count * depth_count
    block_count = pair_blocks.shape[0]
    grid_tiles = TC * col_count
    tile_rows = grid_tiles // row_count
    labels = jnp.zeros((LABEL_ROWS, TILE), jnp.bfloat16)
    labels = labels.at[0, :block_count].set(dest_tile.astype(jnp.bfloat16))
    labels = labels.at[1, :block_count].set(dest_owner[:, 0].astype(jnp.bfloat16))
    piece = jnp.concatenate([pair_blocks.reshape(block_count * TILE, TILE), labels], axis=0)
    pieces = gather_pieces(piece, devices)
    got = pieces[:, block_count * TILE : block_count * TILE + 2, :block_count].astype(jnp.int32)
    row_of = jnp.arange(devices, dtype=jnp.int32)[:, None] // (col_count * depth_count)
    tile_row = row_of * tile_rows + got[:, 0] // TC
    tile_col = got[:, 1] * TC + got[:, 0] % TC
    tile_row, tile_col = tile_row.reshape(-1), tile_col.reshape(-1)
    tiles = tile_row * grid_tiles + tile_col
    total = devices * block_count
    index = jnp.arange(total, dtype=jnp.int32)
    same = tiles[:, None] == tiles[None, :]
    follower = jnp.min(
        jnp.where(same & (index[None, :] > index[:, None]), index[None, :], total), axis=1
    )
    opens = ~jnp.any(same & (index[None, :] < index[:, None]), axis=1)
    special = opens & ((follower < total) | (tile_row == tile_col))
    follower = jnp.where(follower == total, -1, follower)
    chain = jnp.min(
        jnp.where(special[None, :] & (index[None, :] > index[:, None]), index[None, :], total),
        axis=1,
    )
    first = jnp.min(jnp.where(special, index, total))
    place = jnp.stack([lax.axis_index("row"), lax.axis_index("col"), first]).astype(jnp.int32)
    return step_call(
        (tile_row, tile_col, follower, chain, place, chemical_potential, pieces),
        block_count, 1024, row_count, col_count
    )


def step_call(operands, block_count, chunk, row_count, col_count):
    devices = operands[-1].shape[0]
    order = TC * col_count * TILE
    smem = pl.BlockSpec(memory_space=pltpu.SMEM)
    return pl.pallas_call(
        functools.partial(step_kernel, block_count, chunk),
        out_shape=jax.ShapeDtypeStruct((order // row_count, order // col_count), jnp.float32),
        in_specs=[smem] * 6 + [pl.BlockSpec(memory_space=pl.ANY)],
        out_specs=pl.BlockSpec(memory_space=pl.ANY),
        scratch_shapes=[
            pltpu.VMEM((devices, block_count * TILE, TILE), jnp.bfloat16),
            pltpu.VMEM((order, order), jnp.bfloat16),
            pltpu.VMEM((order, order // col_count), jnp.bfloat16),
            pltpu.VMEM((order // row_count, order // col_count), jnp.float32),
            pltpu.SemaphoreType.DMA((8,)),
            pltpu.SemaphoreType.DMA((4,)),
        ],
        compiler_params=pltpu.CompilerParams(vmem_limit_bytes=60 * 2**20),
    )(*operands)


def solution(mesh):
    in_specs = (
        P(("row", "col", "depth"), None, None),
        P(("row", "col", "depth"), None),
        P(("row", "col", "depth")),
        P(),
    )
    out_specs = P("row", "col")
    sizes = mesh.shape
    small = sizes["row"] == 2 and sizes["depth"] == 2 and sizes["col"] == 8
    body = replicated if small else shards
    return jax.shard_map(body, mesh=mesh, in_specs=in_specs, out_specs=out_specs, check_vma=False)
```
